32 devices in a mesh: rows: 8 (over y, x, core), tp: 4 (over z).
Axes of the slice: x: 2, y: 2, z: 4, core: 2. Of those that a mesh axis runs over, the one named last changes fastest.
Arguments:
- first_query: float32 [9216, 9216], P('rows', 'tp'), may hold values from -0.09375 to 0.09375
- second_query: float32 [9216, 9216], P('rows', 'tp'), may hold values from -0.0625 to 0.0625
- first_key: float32 [9216, 9216], P('rows', 'tp'), may hold values from -0.09375 to 0.09375
- second_key: float32 [9216, 9216], P('rows', 'tp'), may hold values from -0.0625 to 0.0625
- first_value: float32 [9216, 9216], P('rows', 'tp'), may hold values from -0.09375 to 0.09375
- second_value: float32 [9216, 9216], P('rows', 'tp'), may hold values from -0.0625 to 0.0625
- mix_share: float32 [9216], P('rows'), may hold values from 0.2 to 0.8
- norm_train: float32 [9216], P(('rows', 'tp')), may hold values from 0.25 to 1.75
- norm_step: float32 [9216], P(('rows', 'tp')), may hold values from -0.3 to 0.3
Outputs:
- serving_query: bfloat16 [9216, 9216], P(None, ('tp', 'rows'))
- serving_key: bfloat16 [9216, 9216], P(None, ('tp', 'rows'))
- serving_value: bfloat16 [9216, 9216], P(None, ('tp', 'rows'))
- scale_query: float32 [9216], P(('tp', 'rows'))
- scale_key: float32 [9216], P(('tp', 'rows'))
- scale_value: float32 [9216], P(('tp', 'rows'))
- serve_norm: bfloat16 [9216], replicated
The draws below stay inside these ranges and needn't reach their ends.
All inputs are finite; a program needn't handle non-finite values.
Results may differ from the reference program's by a relative error of at most 0.001.
Values may be sent and summed in bfloat16 or wider, within the bound.
A program may use at most 192 MiB of HBM per device.

```python
import jax
import jax.numpy as jnp

D_MODEL = 9216
Q_DIM = 9216
KV_DIM = 9216


def with_spikes(entries, own_key, source, target, parts, factor):
    def block_of(dim):
        return (jnp.arange(entries.shape[dim]) // (entries.shape[dim] // parts)).reshape((-1,) + (1,) * (entries.ndim - 1 - dim))

    first = jax.random.permutation(own_key, parts)[block_of(target)]
    other_side = (block_of(target) + parts // 2) % parts
    return jnp.where((block_of(source) == first) | (block_of(source) == other_side), factor * entries, entries)


def block_levels(stream_key, dims, split, low, top_value):
    level, own = 1.0, jax.random.fold_in(stream_key, 6)
    for dim, parts in split:
        draws = jnp.exp(jax.random.uniform(jax.random.fold_in(own, dim), (parts,), jnp.float32, low / len(split), top_value / len(split)))
        level = level * jnp.repeat(draws, dims[dim] // parts).reshape([-1 if axis == dim else 1 for axis in range(len(dims))])
    return level


def scatter_about(stream_key, dims, spread, limit, cuts=(), kind=jnp.bfloat16):
    array = jax.random.normal(stream_key, dims, jnp.float32) * spread
    if len(cuts) > 0:
        array = block_levels(stream_key, dims, cuts, -0.22, 0.18) * array
    return jnp.clip(array, min=-limit, max=limit).astype(kind)


def bell_draw_with(own_key, dims, width, bound, cuts, heavy, held_as=jnp.bfloat16):
    result = width * jax.random.normal(own_key, dims, jnp.float32)
    if cuts:
        result = result * block_levels(own_key, dims, cuts, -0.22, 0.18)
    return jnp.clip(with_spikes(result, jax.random.fold_in(own_key, 3), *heavy), -bound, bound).astype(held_as)


def setup_inputs(seed: int = 0) -> dict:
    streams_of = jax.random.split(jax.random.key(seed), 10)
    return {
        "first_query": bell_draw_with(streams_of[0], (D_MODEL, Q_DIM), D_MODEL ** -0.5, 0.09375, ((0, 8), (1, 4)), (0, 1, 8, 2.0), jnp.float32),
        "second_query": scatter_about(streams_of[1], (D_MODEL, Q_DIM), D_MODEL ** -0.5, 0.0625, ((0, 8), (1, 4)), jnp.float32),
        "first_key": bell_draw_with(streams_of[2], (D_MODEL, KV_DIM), D_MODEL ** -0.5, 0.09375, ((0, 8), (1, 4)), (0, 1, 8, 2.0), jnp.float32),
        "second_key": scatter_about(streams_of[3], (D_MODEL, KV_DIM), D_MODEL ** -0.5, 0.0625, ((0, 8), (1, 4)), jnp.float32),
        "first_value": bell_draw_with(streams_of[4], (D_MODEL, KV_DIM), D_MODEL ** -0.5, 0.09375, ((0, 8), (1, 4)), (0, 1, 8, 2.0), jnp.float32),
        "second_value": scatter_about(streams_of[5], (D_MODEL, KV_DIM), D_MODEL ** -0.5, 0.0625, ((0, 8), (1, 4)), jnp.float32),
        "mix_share": jnp.clip(0.2 + 0.6 * jax.random.uniform(streams_of[6], (D_MODEL,), jnp.float32) ** block_levels(streams_of[6], (D_MODEL,), ((0, 8),), -0.2, 0.2), 0.2, 0.8),
        "norm_train": jnp.clip(1.0 + 0.15 * jax.random.normal(streams_of[7], (D_MODEL,), jnp.float32), 0.25, 1.75),
        "norm_step": jnp.clip(jax.random.uniform(streams_of[8], (D_MODEL,), jnp.float32, -0.3, 0.3) * block_levels(streams_of[8], (D_MODEL,), ((0, 32),), -0.4, 0.0), -0.3, 0.3),
    }


def reference(first_query, second_query, first_key, second_key, first_value, second_value, mix_share, norm_train, norm_step):
    whole_query = mix_share[:, None] * first_query + (1.0 - mix_share[:, None]) * second_query
    whole_key = mix_share[:, None] * first_key + (1.0 - mix_share[:, None]) * second_key
    whole_value = mix_share[:, None] * first_value + (1.0 - mix_share[:, None]) * second_value
    scale_query = jnp.max(jnp.abs(whole_query), axis=0)
    serving_query = (whole_query / scale_query).astype(jnp.bfloat16)
    scale_key = jnp.max(jnp.abs(whole_key), axis=0)
    serving_key = (whole_key / scale_key).astype(jnp.bfloat16)
    scale_value = jnp.max(jnp.abs(whole_value), axis=0)
    serving_value = (whole_value / scale_value).astype(jnp.bfloat16)
    serve_norm = (norm_train + norm_step).astype(jnp.bfloat16)
    return serving_query, serving_key, serving_value, scale_query, scale_key, scale_value, serve_norm
```

```python
import functools
import math

import jax
import jax.numpy as jnp
from jax import lax
from jax.experimental import pallas as pl
from jax.experimental.pallas import tpu as pltpu
from jax.sharding import PartitionSpec as P

MESH = pl.DeviceIdType.MESH
LANES = 128


def kernel(
    n, tp, group, share, deep,
    mix_ref, norm_ref, fq, sq, fk, sk, fv, sv,
    out_q, out_k, out_v, scale_ref, norm_out,
    first, second, whole, narrow, peaks,
    load_sem, peak_send, peak_recv, send_sem, recv_sem, own_sem, norm_send, norm_recv,
):
    row, col = lax.axis_index("rows"), lax.axis_index("tp")
    wide = group * share
    per = n // group
    units = 3 * per
    pairs = ((fq, sq), (fk, sk), (fv, sv))
    outs = (out_q, out_k, out_v)
    count = n * tp
    me = row * tp + col

    def loads(u):
        slot = u % 2
        columns = pl.ds((u % per) * wide, wide)
        a, b = pairs[u // per]
        return (
            pltpu.make_async_copy(a.at[:, columns], first.at[slot], load_sem.at[slot, 0]),
            pltpu.make_async_copy(b.at[:, columns], second.at[slot], load_sem.at[slot, 1]),
        )

    def norm_copy(k, target, origin):
        return pltpu.make_async_remote_copy(
            src_ref=norm_ref.at[0],
            dst_ref=norm_out.at[origin],
            send_sem=norm_send.at[k],
            recv_sem=norm_recv.at[k],
            device_id=(target // tp, target % tp),
            device_id_type=MESH,
        )

    def peak_copy(u, k, target, origin):
        return pltpu.make_async_remote_copy(
            src_ref=peaks.at[u, origin],
            dst_ref=peaks.at[u, origin],
            send_sem=peak_send.at[u, k],
            recv_sem=peak_recv.at[u, k],
            device_id=(target, col),
            device_id_type=MESH,
        )

    def share_copy(m, k, target, origin, u, j):
        return pltpu.make_async_remote_copy(
            src_ref=narrow.at[u, pl.ds(pl.multiple_of(j * share, share), share), :],
            dst_ref=outs[m].at[:, pl.ds(pl.multiple_of(origin * deep, LANES), deep)],
            send_sem=send_sem.at[m, k],
            recv_sem=recv_sem.at[m, k],
            device_id=(target, col),
            device_id_type=MESH,
        )

    def own_copy(u, j):
        m = u // per
        return pltpu.make_async_copy(
            narrow.at[u, pl.ds(pl.multiple_of(j * share, share), share), :],
            outs[m].at[:, pl.ds(pl.multiple_of(row * deep, LANES), deep)],
            own_sem.at[m],
        )

    def mix(u):
        slot = u % 2

        def step(i, top):
            rows = pl.ds(pl.multiple_of(i * 16, 16), 16)
            part = jnp.concatenate([mix_ref[rows, :]] * (wide // LANES), axis=1)
            value = part * first[slot, rows, :] + (1.0 - part) * second[slot, rows, :]
            whole[slot, rows, :] = value
            size = jnp.abs(value)
            return jnp.maximum(top, jnp.maximum(size[:8], size[8:]))

        top = lax.fori_loop(0, deep // 16, step, jnp.zeros((8, wide), jnp.float32))
        peaks[u, row] = jnp.max(top, axis=0, keepdims=True)

    def narrow_down(u):
        slot = u % 2
        scale = jnp.max(peaks[u], axis=0)
        scale_ref[u] = scale
        inverse = 1.0 / scale

        def step(i, carry):
            rows = pl.ds(pl.multiple_of(i * LANES, LANES), LANES)
            for c in range(wide // LANES):
                cut = slice(c * LANES, (c + 1) * LANES)
                value = whole[slot, rows, cut] * inverse[:, cut]
                narrow[u, cut, rows] = value.T.astype(jnp.bfloat16)
            return carry

        lax.fori_loop(0, deep // LANES, step, 0)

    def each(lower, upper, body):
        def step(k, carry):
            body(k)
            return carry

        lax.fori_loop(lower, upper, step, 0)

    for u in range(min(2, units)):
        for copy in loads(u):
            copy.start()
    for u in range(units + 1):
        if u < units:
            for copy in loads(u):
                copy.wait()
            mix(u)
            if u + 2 < units:
                for copy in loads(u + 2):
                    copy.start()
            each(1, n, lambda k: peak_copy(u, k, (row + k) % n, row).start())
        if u == 0:
            each(1, count, lambda k: norm_copy(k, (me + k) % count, me).start())
            norm_out[me] = norm_ref[0]
        if u >= 1:
            v = u - 1
            each(1, n, lambda k: peak_copy(v, k, row, (row + n - k) % n).wait_recv())
            narrow_down(v)
            base = (v % per) * group

            def send(j):
                place = (row + j) % group
                target = base + place
                k = (target + n - row) % n

                @pl.when(target != row)
                def _():
                    share_copy(v // per, k, target, row, v, place).start()

                @pl.when(target == row)
                def _():
                    own_copy(v, place).start()

            each(0, group, send)

    each(1, count, lambda k: norm_copy(k, me, (me + count - k) % count).wait_recv())
    each(1, count, lambda k: norm_copy(k, me, me).wait_send())
    for u in range(units):
        each(1, n, lambda k: peak_copy(u, k, row, row).wait_send())
    for m in range(3):
        pltpu.make_async_copy(
            narrow.at[0, pl.ds(0, share), :], outs[m].at[:, pl.ds(0, deep)], own_sem.at[m]
        ).wait()
        each(1, n, lambda k: share_copy(m, k, row, (row + n - k) % n, m * per, 0).wait_recv())
        each(1, n, lambda k: share_copy(m, k, row, row, m * per, 0).wait_send())


def plain_device(
    first_query,
    second_query,
    first_key,
    second_key,
    first_value,
    second_value,
    mix_share,
    norm_train,
    norm_step,
):
    whole_query = mix_share[:, None] * first_query + (1.0 - mix_share[:, None]) * second_query
    whole_key = mix_share[:, None] * first_key + (1.0 - mix_share[:, None]) * second_key
    whole_value = mix_share[:, None] * first_value + (1.0 - mix_share[:, None]) * second_value
    scale_query, scale_key, scale_value = lax.pmax(
        (
            jnp.max(jnp.abs(whole_query), axis=0),
            jnp.max(jnp.abs(whole_key), axis=0),
            jnp.max(jnp.abs(whole_value), axis=0),
        ),
        "rows",
    )
    narrow_query, narrow_key, narrow_value = (
        (whole_query / scale_query).astype(jnp.bfloat16),
        (whole_key / scale_key).astype(jnp.bfloat16),
        (whole_value / scale_value).astype(jnp.bfloat16),
    )
    serving_query, serving_key, serving_value = (
        lax.all_to_all(narrow_query, "rows", split_axis=1, concat_axis=0, tiled=True),
        lax.all_to_all(narrow_key, "rows", split_axis=1, concat_axis=0, tiled=True),
        lax.all_to_all(narrow_value, "rows", split_axis=1, concat_axis=0, tiled=True),
    )
    place = lax.axis_index("rows")
    scale_query = lax.dynamic_slice_in_dim(
        scale_query, place * serving_query.shape[1], serving_query.shape[1]
    )
    scale_key = lax.dynamic_slice_in_dim(
        scale_key, place * serving_key.shape[1], serving_key.shape[1]
    )
    scale_value = lax.dynamic_slice_in_dim(
        scale_value, place * serving_value.shape[1], serving_value.shape[1]
    )
    serve_norm = lax.all_gather(
        (norm_train + norm_step).astype(jnp.bfloat16), ("rows", "tp"), axis=0, tiled=True
    )
    return (
        serving_query,
        serving_key,
        serving_value,
        scale_query,
        scale_key,
        scale_value,
        serve_norm,
    )


def per_device(n, tp, fq, sq, fk, sk, fv, sv, mix_share, norm_train, norm_step):
    deep, columns = fq.shape
    share = columns // n
    group = LANES // math.gcd(share, LANES)
    if deep % LANES or share % 16 or n % group:
        return plain_device(fq, sq, fk, sk, fv, sv, mix_share, norm_train, norm_step)
    wide = group * share
    units = 3 * (n // group)
    count = n * tp
    length = norm_train.shape[0]
    room = -(-length // LANES) * LANES
    mix = jnp.broadcast_to(mix_share[:, None], (deep, LANES))
    norm = jnp.pad(norm_train + norm_step, (0, room - length)).reshape(1, 1, room)
    vmem = pl.BlockSpec(memory_space=pltpu.VMEM)
    hbm = pl.BlockSpec(memory_space=pl.ANY)
    out = jax.ShapeDtypeStruct((share, n * deep), jnp.bfloat16)
    dma = pltpu.SemaphoreType.DMA
    q, k, v, scales, norms = pl.pallas_call(
        functools.partial(kernel, n, tp, group, share, deep),
        name="mix_and_spread",
        out_shape=(
            out,
            out,
            out,
            jax.ShapeDtypeStruct((units, 1, wide), jnp.float32),
            jax.ShapeDtypeStruct((count, 1, room), jnp.float32),
        ),
        in_specs=[vmem, vmem] + [hbm] * 6,
        out_specs=(hbm, hbm, hbm, vmem, vmem),
        scratch_shapes=[
            pltpu.VMEM((2, deep, wide), jnp.float32),
            pltpu.VMEM((2, deep, wide), jnp.float32),
            pltpu.VMEM((2, deep, wide), jnp.float32),
            pltpu.VMEM((units, wide, deep), jnp.bfloat16),
            pltpu.VMEM((units, n, 1, wide), jnp.float32),
            dma((2, 2)),
            dma((units, n)),
            dma((units, n)),
            dma((3, n)),
            dma((3, n)),
            dma((3,)),
            dma((count,)),
            dma((count,)),
        ],
        compiler_params=pltpu.CompilerParams(
            has_side_effects=True, vmem_limit_bytes=60 * 1024 * 1024
        ),
    )(mix, norm, fq, sq, fk, sk, fv, sv)
    scales = scales.reshape(3, columns)
    place = lax.axis_index("rows") * share
    own = lax.dynamic_slice(scales, (0, place), (3, share))
    serve_norm = norms[:, 0, :length].reshape(count * length).astype(jnp.bfloat16)
    return q.T, k.T, v.T, own[0], own[1], own[2], serve_norm


def solution(mesh):
    return jax.shard_map(
        functools.partial(per_device, mesh.shape["rows"], mesh.shape["tp"]),
        mesh=mesh,
        in_specs=(P("rows", "tp"),) * 6 + (P("rows"), P(("rows", "tp")), P(("rows", "tp"))),
        out_specs=(P(None, ("tp", "rows")),) * 3 + (P(("tp", "rows")),) * 3 + (P(),),
        check_vma=False,
    )
```
